32 devices in a mesh: pairs: 8 (over z, x), hours: 4 (over y, core).
Axes of the slice: x: 2, y: 2, z: 4, core: 2. Of those that a mesh axis runs over, the one named last changes fastest.
Arguments:
- records: bfloat16 [1024, 4, 3600], P('pairs', 'hours'), may hold values from -100 to 100
- usable: int32 [1024, 4], P('pairs', 'hours'), may hold values from 0 to 1, as said below
- pair_blocks: int32 [8, 2], P('pairs'), may hold values from 0 to 7
Outputs:
- correlations: float32 [8, 128, 128, 256], P('pairs', 'hours')
The draws below stay inside these ranges and needn't reach their ends.
Inputs may be any that keep to these rules, and one draw needn't show every extreme that they name: Some stations are usable in no hour at all. `pair_blocks`: each row names two station blocks; a block may appear in many rows and both entries may be equal.
All inputs are finite; a program needn't handle non-finite values.
Results may differ from the reference program's by a relative error of at most 0.0071.
Values may be sent and summed in bfloat16 or wider, within the bound.
A program may use at most 128 MiB of HBM per device.

```python
import math
import jax
import jax.numpy as jnp
import numpy as np
from jax import lax

SB = 128
L = 3600
F = 512
W = 32
F0 = 64
LAGS = 256
STATIONS = 1024
HOURS = 4
PAIRS_ALL = 8


def draw_records(key, part):
    key_scale, key_base = jax.random.split(key, 2)
    station_scale = jnp.exp(jax.random.uniform(key_scale, (STATIONS, 1, 1), jnp.float32, 0.0, math.log(10.0)))
    base = jax.random.normal(key_base, (STATIONS, HOURS, L), jnp.float32)
    return (station_scale * base).astype(jnp.bfloat16)


def draw_usable(key, part):
    key_draws, key_dead = jax.random.split(key, 2)
    hour_rank = jnp.arange(HOURS, dtype=jnp.int32)
    threshold = 30 + 65 * hour_rank // max(HOURS - 1, 1)
    rolls = jax.random.randint(key_draws, (STATIONS, HOURS), 0, 100)
    alive = jax.random.randint(key_dead, (STATIONS, 1), 0, 16) != 0
    return jnp.where((rolls < threshold[None, :]) & alive, 1, 0).astype(jnp.int32)


def with_ends(entries, rng, low, top_value):
    shape = entries.shape
    spot = [jax.random.randint(jax.random.fold_in(rng, axis), (), 0, shape[axis]) for axis in range(len(shape))]
    entries = entries.at[tuple(spot)].set(low)
    longest = shape.index(max(shape))
    spot[longest] = (spot[longest] + 1) % shape[longest]
    return entries.at[tuple(spot)].set(top_value)


def rank_table(count, skew):
    loads = [(1 << 20) // math.isqrt(standing ** skew) + 1 for standing in range(1, count + 1)]
    width = 1 + sum(loads) // (1 << 30)
    return np.cumsum(np.array([max(1, weight // width) for weight in loads]))


def skewed_ids(stream_key, dims, count, skew):
    listing = rank_table(count, skew)
    pick = jax.random.randint(jax.random.fold_in(stream_key, 1), dims, 0, int(listing[count - 1]))
    rank = jnp.searchsorted(jnp.asarray(listing, jnp.int32), pick, side="right")
    return jax.random.permutation(jax.random.fold_in(stream_key, 2), count)[rank].astype(jnp.int32)


def setup_inputs(seed: int = 0) -> dict:
    key_of = jax.random.split(jax.random.key(seed), 4)
    return {
        "records": draw_records(jax.random.fold_in(key_of[3], 71), 0),
        "usable": draw_usable(jax.random.fold_in(key_of[3], 71), 0),
        "pair_blocks": with_ends(skewed_ids(key_of[2], (PAIRS_ALL, 2), STATIONS // SB, 2), jax.random.fold_in(key_of[2], 3), 0, (STATIONS // SB) - 1).astype(jnp.int32),
    }


def spectrum_table():
    extent = F + 2 * W
    freq_bins = F0 - W + jnp.arange(extent, dtype=jnp.int32)
    samples = jnp.arange(L, dtype=jnp.int32)
    phases = samples[:, None] * freq_bins[None, :] % L
    angles = 2.0 * math.pi / L * phases.astype(jnp.float32)
    factor = 1.0 / math.sqrt(L)
    return jnp.concatenate([jnp.cos(angles) * factor, -jnp.sin(angles) * factor], axis=1).astype(jnp.bfloat16)

def smoothing_matrix():
    extent = F + 2 * W
    source = jnp.arange(extent, dtype=jnp.int32)[:, None]
    target = jnp.arange(F, dtype=jnp.int32)[None, :]
    spacing = source - target
    within = (spacing >= 0) & (spacing <= 2 * W)
    return jnp.where(within, jnp.float32(1.0 / (2 * W + 1)), jnp.float32(0.0)).astype(jnp.float32)

def lag_weights():
    freq_bins = F0 + jnp.arange(F, dtype=jnp.int32)
    shifts = jnp.arange(LAGS, dtype=jnp.int32) - LAGS // 2
    phases = freq_bins[:, None] * shifts[None, :] % L
    angles = 2.0 * math.pi / L * phases.astype(jnp.float32)
    factor = 1.0 / math.sqrt(F)
    return jnp.concatenate([jnp.cos(angles) * factor, -jnp.sin(angles) * factor], axis=0).astype(jnp.bfloat16)

def whiten(signal, usable_flags):
    station_rows, hour_count = (signal.shape[0], signal.shape[1])
    flat = signal.reshape(station_rows * hour_count, L).astype(jnp.float32)
    spectra = jnp.dot(flat, spectrum_table().astype(jnp.float32), precision=lax.Precision.HIGHEST)
    extent = F + 2 * W
    real_part = spectra[:, :extent]
    imag_part = spectra[:, extent:]
    power = real_part * real_part + imag_part * imag_part
    smooth = jnp.dot(power, smoothing_matrix(), precision=lax.Precision.HIGHEST)
    weight = usable_flags.reshape(station_rows * hour_count, 1).astype(jnp.float32) / jnp.sqrt(smooth + 1e-05)
    whitened = jnp.concatenate([real_part[:, W:W + F] * weight, imag_part[:, W:W + F] * weight], axis=1)
    return whitened.astype(jnp.bfloat16).reshape(station_rows, hour_count, 2 * F)

def hour_cross(first_hour, second_hour):
    first_real = first_hour[:, :F].astype(jnp.float32)
    first_imag = first_hour[:, F:].astype(jnp.float32)
    second_real = second_hour[:, :F].astype(jnp.float32)
    second_imag = second_hour[:, F:].astype(jnp.float32)
    cross_real = first_real[:, None, :] * second_real[None, :, :] + first_imag[:, None, :] * second_imag[None, :, :]
    cross_imag = first_imag[:, None, :] * second_real[None, :, :] - first_real[:, None, :] * second_imag[None, :, :]
    return jnp.concatenate([cross_real, cross_imag], axis=2).astype(jnp.bfloat16)

def correlate(first_block, second_block, first_flags, second_flags, weights):
    first_rows = first_block.shape[0]
    second_rows = second_block.shape[0]
    weights_wide = weights.astype(jnp.float32)

    def add_hour(hour_step, running):
        first_hour = lax.dynamic_index_in_dim(first_block, hour_step, 1, keepdims=False)
        second_hour = lax.dynamic_index_in_dim(second_block, hour_step, 1, keepdims=False)
        cross = hour_cross(first_hour, second_hour).astype(jnp.float32)
        lagged = jnp.dot(cross.reshape(first_rows * second_rows, 2 * F), weights_wide, precision=lax.Precision.HIGHEST)
        return running + lagged.reshape(first_rows, second_rows, LAGS)
    stacks = lax.fori_loop(0, first_block.shape[1], add_hour, jnp.zeros((first_rows, second_rows, LAGS), jnp.float32))
    counts = jnp.dot(first_flags.astype(jnp.float32), second_flags.astype(jnp.float32).T, precision=lax.Precision.HIGHEST)
    return (stacks, counts)

def reference(records, usable, pair_blocks):
    whitened = whiten(records, usable)
    weights = lag_weights()

    def one_tile(blocks_pair):
        first_start = (blocks_pair[0] * SB).astype(jnp.int32)
        second_start = (blocks_pair[1] * SB).astype(jnp.int32)
        first_block = lax.dynamic_slice_in_dim(whitened, first_start, SB, 0)
        second_block = lax.dynamic_slice_in_dim(whitened, second_start, SB, 0)
        first_flags = lax.dynamic_slice_in_dim(usable, first_start, SB, 0)
        second_flags = lax.dynamic_slice_in_dim(usable, second_start, SB, 0)
        stacks, counts = correlate(first_block, second_block, first_flags, second_flags, weights)
        return stacks / jnp.maximum(counts, 1.0)[:, :, None]
    return lax.map(one_tile, pair_blocks)
```

```python
import functools
import math

import jax
import jax.numpy as jnp
import numpy as np
from jax import lax
from jax.experimental import pallas as pl
from jax.experimental.pallas import tpu as pltpu
from jax.sharding import PartitionSpec as P

L = 3600
F = 512
W = 32
F0 = 64
LAGS = 256
EXTENT = F + 2 * W
HALF = L // 2
HE = EXTENT // 2
HF = F // 2
CORES = 2
MESH = pl.DeviceIdType.MESH


def cos_sin(phases, length, scale):
    angles = np.float32(2.0 * math.pi / length) * (phases % length).astype(np.float32)
    wide = angles.astype(np.float64)
    scale = np.float32(scale)
    return np.cos(wide).astype(np.float32) * scale, -np.sin(wide).astype(np.float32) * scale


CHUNK = 256
CHUNKS = F // CHUNK


def spectrum_tables():
    bins = F0 - W + np.arange(EXTENT)
    c, q = cos_sin(bins[:, None] * np.arange(HALF)[None, :], L, 1.0 / math.sqrt(L))
    even = np.concatenate([c[0::2], q[0::2]], axis=0)
    odd = np.concatenate([c[1::2], q[1::2]], axis=0)
    return even.astype(jnp.bfloat16), odd.astype(jnp.bfloat16)


def window_ones():
    source = np.concatenate([np.arange(0, EXTENT, 2), np.arange(1, EXTENT, 2)])
    target = np.concatenate([np.arange(0, F, 2), np.arange(1, F, 2)])
    gap = source[None, :] - target[:, None]
    return ((gap >= 0) & (gap <= 2 * W)).astype(np.float32).astype(jnp.bfloat16)


def lag_weights():
    order = np.concatenate([np.arange(0, F, 2), np.arange(1, F, 2)])
    shifts = np.arange(LAGS) - LAGS // 2
    c, s = cos_sin((F0 + order)[:, None] * shifts[None, :], L, 1.0 / math.sqrt(F))
    pieces = []
    for k in range(0, F, CHUNK):
        pieces += [c[k : k + CHUNK], s[k : k + CHUNK]]
    return np.concatenate(pieces, axis=0).astype(jnp.bfloat16)


def split_hi_lo(value):
    high = value.astype(jnp.bfloat16)
    low = (value - high.astype(jnp.float32)).astype(jnp.bfloat16)
    return jnp.concatenate([high, low], axis=1)


def whiten_kernel(
    x_ref, use_ref, even_hbm, odd_hbm, ones_hbm, out_ref, mark_ref, even, odd, ones, sem
):
    stations = x_ref.shape[1]
    loads = [
        pltpu.make_async_copy(src, dst, sem.at[k])
        for k, (src, dst) in enumerate(((even_hbm, even), (odd_hbm, odd), (ones_hbm, ones)))
    ]
    for load in loads:
        load.start()
    flags = use_ref[...].astype(jnp.float32)
    mark_ref[...] = jnp.broadcast_to(flags, mark_ref.shape).astype(jnp.bfloat16)
    early = x_ref[:HALF].astype(jnp.float32)
    late = x_ref[HALF:].astype(jnp.float32)

    def transform(load, table, signal):
        signal = split_hi_lo(signal)
        load.wait()
        both = jnp.dot(table[...], signal, preferred_element_type=jnp.float32)
        both = both[:, :stations] + both[:, stations:]
        return both[:HE], both[HE:]

    re_even, im_even = transform(loads[0], even, early + late)
    re_odd, im_odd = transform(loads[1], odd, early - late)
    power = jnp.concatenate(
        [re_even * re_even + im_even * im_even, re_odd * re_odd + im_odd * im_odd], axis=0
    )
    loads[2].wait()
    total = jnp.dot(ones[...], split_hi_lo(power), preferred_element_type=jnp.float32)
    smooth = (total[:, :stations] + total[:, stations:]) * jnp.float32(1.0 / (2 * W + 1))
    weight = flags / jnp.sqrt(smooth + 1e-05)
    w2 = W // 2
    for k in range(CHUNKS):
        at = k * CHUNK
        real, imag = (re_even, im_even) if at < HF else (re_odd, im_odd)
        inner = w2 + at % HF
        scale = weight[at : at + CHUNK]
        out_ref[k, :, :CHUNK] = (real[inner : inner + CHUNK] * scale).T.astype(jnp.bfloat16)
        out_ref[k, :, CHUNK:] = (imag[inner : inner + CHUNK] * scale).T.astype(jnp.bfloat16)


def exchange_kernel(
    pairs, width, hours, pair_ref, ask_ref, w_ref, f_ref, bj, bi, bf,
    *scratch,
):
    rows = w_ref.shape[1]
    part = rows // hours
    span_rows = rows // SPLIT
    units = CHUNKS * SPLIT
    g = scratch[:units]
    (
        gf, sj, si, sf, hand, hand_f, asks, zx_send, zx_recv, j_send, j_recv, relay_send,
        i_send, i_recv, f_send, f_recv, local_sem, i_local, a_send, a_recv, x_send, x_recv,
    ) = scratch[units:]
    depth = pairs // width
    p = lax.axis_index("pairs")
    me = lax.axis_index("hours")
    z, x = p // width, p % width
    y, core = me // CORES, me % CORES
    partner = y * CORES + (1 - core)
    flags_unit = units

    def place(u):
        return u // SPLIT, pl.ds((u % SPLIT) * span_rows, span_rows)

    def beside(k):
        return z * width + (x + k) % width

    steps = (
        (z + 1 < depth, p + width),
        (z > 0, p - width),
    )

    barrier = pltpu.get_barrier_semaphore()
    for exists, target in steps:
        @pl.when(exists)
        def _(target=target):
            pl.semaphore_signal(barrier, inc=1, device_id={"pairs": target}, device_id_type=MESH)
    for k in range(1, hours):
        pl.semaphore_signal(
            barrier, inc=1, device_id={"hours": (me + k) % hours}, device_id_type=MESH
        )
    for k in range(1, width):
        pl.semaphore_signal(
            barrier, inc=1, device_id={"pairs": beside(k)}, device_id_type=MESH
        )
    near = sum(e.astype(jnp.int32) for e, _ in steps)
    pl.semaphore_wait(barrier, near + hours - 1 + width - 1)

    pending = []

    def slot(b, u):
        return gf.at[b // width] if u == flags_unit else g[u].at[b // width]

    def own(u):
        return f_ref if u == flags_unit else w_ref.at[place(u)]

    def forward(cond, b, u, way, is_own=False):
        exists, target = steps[way]
        both = exists if cond is None else jnp.logical_and(cond, exists)

        def make():
            return pltpu.make_async_remote_copy(
                src_ref=own(u) if is_own else slot(b, u),
                dst_ref=slot(b, u),
                send_sem=zx_send.at[way, b // width, u],
                recv_sem=zx_recv.at[b // width, u],
                device_id={"pairs": target},
                device_id_type=MESH,
            )

        @pl.when(both)
        def _():
            make().start()
        pending.append((both, make))

    def arrived(b, u):
        pltpu.make_async_remote_copy(
            src_ref=slot(b, u), dst_ref=slot(b, u), send_sem=zx_send.at[0, b // width, u],
            recv_sem=zx_recv.at[b // width, u], device_id={"pairs": p}, device_id_type=MESH,
        ).wait_recv()

    def send_own(u):
        for way in range(4):
            forward(None, p, u, way, is_own=True)

    keep = [
        pltpu.make_async_copy(own(u), slot(p, u), local_sem.at[u]) for u in range(units + 1)
    ]
    for copy in keep:
        copy.start()

    def gather_z(u, d):
        for way, b, cond in (
            (0, p - d * width, z - d >= 0),
            (1, p + d * width, z + d < depth),
        ):
            @pl.when(cond)
            def _(b=b):
                arrived(b, u)
            forward(cond, b, u, way)

    def crossing(k, u):
        hand_of = hand_f.at[k - 1] if u == flags_unit else hand.at[k - 1, u]
        dst = gf if u == flags_unit else g[u]
        return pltpu.make_async_remote_copy(
            src_ref=hand_of,
            dst_ref=dst.at[pl.ds(depth + 2 * (width - k - 1), 2)],
            send_sem=x_send.at[k - 1, u],
            recv_sem=x_recv.at[width - k - 1, u],
            device_id={"pairs": beside(k)},
            device_id_type=MESH,
        )

    def offer(u):
        keep[u].wait()
        pool = gf if u == flags_unit else g[u]
        for k in range(1, width):
            for s in range(2):
                asked = asks[k - 1, s, 0:1, 0:1].astype(jnp.float32)
                picked = None
                for zz in range(depth):
                    mark = jnp.where(asked == (zz * width + x).astype(jnp.float32), 1.0, 0.0)
                    term = pool[zz].astype(jnp.float32) * mark
                    picked = term if picked is None else picked + term
                if u == flags_unit:
                    hand_f[k - 1, s] = picked.astype(jnp.bfloat16)
                else:
                    hand[k - 1, u, s] = picked.astype(jnp.bfloat16)
            crossing(k, u).start()

    def chosen(s):
        b = pair_ref[0, s]
        away = lax.rem(lax.rem(b, width) - x + width, width)
        return jnp.where(away == 0, b // width, depth + 2 * (away - 1) + s)

    late = []
    local = []

    def remote(src, dst, send_sem, recv_sem, target):
        copy = pltpu.make_async_remote_copy(
            src_ref=src, dst_ref=dst, send_sem=send_sem, recv_sem=recv_sem,
            device_id={"hours": target}, device_id_type=MESH,
        )
        copy.start()
        late.append(copy)

    def stay(src, dst, sem):
        copy = pltpu.make_async_copy(src, dst, sem)
        copy.start()
        local.append(copy)

    def share(u):
        for k in range(1, width):
            crossing(width - k, u).wait_recv()
        if u == flags_unit:
            sf[0] = gf[chosen(0)]
            sf[1] = gf[chosen(1)]
            for k in range(1, hours):
                remote(sf, bf.at[me], f_send.at[k], f_recv.at[me], (me + k) % hours)
            stay(sf, bf.at[me], local_sem.at[units + 1])
            return
        c, span = place(u)
        sj[u] = g[u][chosen(1)]
        si[u] = g[u][chosen(0)]
        for k in range(1, hours // CORES):
            target = ((y + k) % (hours // CORES)) * CORES + core
            remote(sj.at[u], bj.at[me, c, span], j_send.at[k, u], j_recv.at[me, u], target)
        remote(sj.at[u], bj.at[me, c, span], j_send.at[0, u], j_recv.at[me, u], partner)
        stay(sj.at[u], bj.at[me, c, span], local_sem.at[units + 2 + u])
        share_hours = hours // SPLIT
        for k in range(share_hours):
            peer = (u % SPLIT) * share_hours + k
            rows_of = si.at[u, pl.ds(k * part, part)]

            def make(peer=peer, rows_of=rows_of):
                return pltpu.make_async_remote_copy(
                    src_ref=rows_of, dst_ref=bi.at[me, c], send_sem=i_send.at[c, peer],
                    recv_sem=i_recv.at[me, c], device_id={"hours": peer}, device_id_type=MESH,
                )

            @pl.when(me != peer)
            def _(make=make):
                make().start()
            pending.append((me != peer, make))

            @pl.when(me == peer)
            def _(rows_of=rows_of):
                pltpu.make_async_copy(rows_of, bi.at[me, c], i_local.at[c]).start()

    def got(sem, ref):
        pltpu.make_async_remote_copy(
            src_ref=ref, dst_ref=ref, send_sem=sem, recv_sem=sem,
            device_id={"hours": me}, device_id_type=MESH,
        ).wait_recv()

    def relay(u):
        c, span = place(u)
        for k in range(1, hours // CORES):
            peer = ((y + k) % (hours // CORES)) * CORES + core
            piece = bj.at[peer, c, span]
            got(j_recv.at[peer, u], piece)
            remote(piece, piece, relay_send.at[k, u], j_recv.at[peer, u], partner)

    def asking(k):
        return pltpu.make_async_remote_copy(
            src_ref=ask_ref, dst_ref=asks.at[width - k - 1], send_sem=a_send.at[k - 1],
            recv_sem=a_recv.at[width - k - 1], device_id={"pairs": beside(k)},
            device_id_type=MESH,
        )

    order = [flags_unit] + list(range(units))
    for k in range(1, width):
        asking(k).start()
    for t in range(len(order) + depth + 3):
        if t < len(order):
            for way in range(2):
                forward(None, p, order[t], way, is_own=True)
        for d in range(1, depth):
            if 0 <= t - d < len(order):
                gather_z(order[t - d], d)
        if t == depth - 1:
            for k in range(1, width):
                asking(width - k).wait_recv()
        if 0 <= t - depth + 1 < len(order):
            offer(order[t - depth + 1])
        if 0 <= t - depth - 1 < len(order):
            share(order[t - depth - 1])
        if 1 <= t - depth - 2 < len(order):
            relay(order[t - depth - 2])

    for k in range(1, width):
        asking(k).wait_send()
        for u in range(units + 1):
            crossing(k, u).wait_send()
    for u in range(units):
        c, span = place(u)
        for k in range(hours // CORES):
            peer = ((y + k) % (hours // CORES)) * CORES + (1 - core)
            got(j_recv.at[peer, u], bj.at[peer, c, span])
    for k in range(1, hours):
        peer = (me + k) % hours
        for c in range(CHUNKS):
            got(i_recv.at[peer, c], bi.at[peer, c])
        got(f_recv.at[peer], bf.at[peer])
    for copy in local:
        copy.wait()
    for c in range(CHUNKS):
        pltpu.make_async_copy(bi.at[me, c], bi.at[me, c], i_local.at[c]).wait()
    for cond, make in pending:
        @pl.when(cond)
        def _(make=make):
            make().wait_send()
    for copy in late:
        copy.wait_send()


SPLIT = 4


def exchange(pair_blocks, asks, whitened, marks, pairs, width, hours):
    rows, cols = whitened.shape[1:]
    part = rows // hours
    units = CHUNKS * SPLIT
    any_space = pl.BlockSpec(memory_space=pl.ANY)
    dma = pltpu.SemaphoreType.DMA
    groups = hours // CORES
    depth = pairs // width
    slots = depth + 2 * (width - 1)
    return pl.pallas_call(
        functools.partial(exchange_kernel, pairs, width, hours),
        out_shape=(
            jax.ShapeDtypeStruct((hours, CHUNKS, rows, cols), jnp.bfloat16),
            jax.ShapeDtypeStruct((hours, CHUNKS, part, cols), jnp.bfloat16),
            jax.ShapeDtypeStruct((hours, 2) + marks.shape, jnp.bfloat16),
        ),
        in_specs=[pl.BlockSpec(memory_space=pltpu.SMEM), any_space, any_space, any_space],
        out_specs=(any_space, any_space, any_space),
        scratch_shapes=[pltpu.VMEM((slots, rows // SPLIT, cols), jnp.bfloat16)] * units + [
            pltpu.VMEM((slots,) + marks.shape, jnp.bfloat16),
            pltpu.VMEM((units, rows // SPLIT, cols), jnp.bfloat16),
            pltpu.VMEM((units, rows // SPLIT, cols), jnp.bfloat16),
            pltpu.VMEM((2,) + marks.shape, jnp.bfloat16),
            pltpu.VMEM((width - 1, units, 2, rows // SPLIT, cols), jnp.bfloat16),
            pltpu.VMEM((width - 1, 2) + marks.shape, jnp.bfloat16),
            pltpu.VMEM((width - 1,) + asks.shape, asks.dtype),
            dma((2, depth, units + 1)),
            dma((depth, units + 1)),
            dma((groups, units)),
            dma((hours, units)),
            dma((groups, units)),
            dma((CHUNKS, hours)),
            dma((hours, CHUNKS)),
            dma((hours,)),
            dma((hours,)),
            dma((2 * units + 2,)),
            dma((CHUNKS,)),
            dma((width - 1,)),
            dma((width - 1,)),
            dma((width - 1, units + 1)),
            dma((width - 1, units + 1)),
        ],
        compiler_params=pltpu.CompilerParams(
            collective_id=0, has_side_effects=True, vmem_limit_bytes=32 << 20
        ),
        name="exchange",
    )(pair_blocks, asks, whitened, marks)


GROUP = 8
SUB = 2
BLOCK = 8


def stack_kernel(
    hours, me_ref, bi_ref, bj_ref, bf_ref, g_ref, out_ref, af, heads, recip, *cross
):
    step = pl.program_id(0)
    rows = bj_ref.shape[2]
    first_rows = bi_ref.shape[2]
    f32 = jnp.float32

    @pl.when(step == 0)
    def _():
        af[...] = bi_ref[...].astype(f32)
        first = bf_ref[:, 0, 0, :]
        second = bf_ref[:, 1, 0, :]
        counts = lax.dot_general(
            second, first, (((0,), (0,)), ((), ())), preferred_element_type=f32
        )
        recip[...] = 1.0 / jnp.maximum(counts, 1.0)

    offset = me_ref[0] * first_rows + step * GROUP
    scale = pltpu.roll(recip[...], (rows - offset) % rows, 1)
    at_rows = pl.ds(pl.multiple_of(step * GROUP, GROUP), GROUP)
    for h in range(hours):
        for c in range(CHUNKS):
            ar = af[h, c, at_rows, :CHUNK]
            ai = af[h, c, at_rows, CHUNK:]
            for k, value in enumerate((ar, ai)):
                for a in range(GROUP):
                    heads[a, c, h, k] = jnp.broadcast_to(
                        value[a : a + 1], (BLOCK, CHUNK)
                    ).astype(jnp.bfloat16)

    for sub in range(GROUP // SUB):
        buf = cross[sub]
        for c in range(CHUNKS):
            lo = 2 * CHUNK * c
            hi = lo + CHUNK
            for r in range(0, rows, BLOCK):
                tails = []
                for h in range(hours):
                    tails.append(
                        (
                            bj_ref[h, c, r : r + BLOCK, :CHUNK],
                            bj_ref[h, c, r : r + BLOCK, CHUNK:],
                        )
                    )
                for a in range(SUB):
                    real = imag = None
                    for h in range(hours):
                        ar, ai = heads[sub * SUB + a, c, h, 0], heads[sub * SUB + a, c, h, 1]
                        br, bm = tails[h]
                        re = ar * br + ai * bm
                        im = ai * br - ar * bm
                        real = re if real is None else real + re
                        imag = im if imag is None else imag + im
                    at = a * rows + r
                    buf[at : at + BLOCK, lo:hi] = real
                    buf[at : at + BLOCK, hi : hi + CHUNK] = imag
        lagged = jnp.dot(buf[...], g_ref[...], preferred_element_type=f32)
        for a in range(SUB):
            k = sub * SUB + a
            out_ref[0, k] = lagged[a * rows : (a + 1) * rows] * scale[:, k : k + 1]


def stack(me, bi, bj, bf, weights):
    hours, _, first_rows, cols = bi.shape
    rows = bj.shape[2]
    full = lambda a: pl.BlockSpec(a.shape, lambda i, *_: (0,) * a.ndim, pipeline_mode=pl.Buffered(1))
    return pl.pallas_call(
        functools.partial(stack_kernel, hours),
        grid_spec=pltpu.PrefetchScalarGridSpec(
            num_scalar_prefetch=1,
            grid=(first_rows // GROUP,),
            in_specs=[full(bi), full(bj), full(bf), full(weights)],
            out_specs=pl.BlockSpec((1, GROUP, rows, LAGS), lambda i, *_: (0, i, 0, 0)),
            scratch_shapes=[
                pltpu.VMEM((hours, CHUNKS, first_rows, cols), jnp.float32),
                pltpu.VMEM((GROUP, CHUNKS, hours, 2, BLOCK, CHUNK), jnp.bfloat16),
                pltpu.VMEM((rows, rows), jnp.float32),
            ]
            + [pltpu.VMEM((SUB * rows, 2 * F), jnp.bfloat16)] * (GROUP // SUB),
        ),
        out_shape=jax.ShapeDtypeStruct((1, first_rows, rows, LAGS), jnp.float32),
        compiler_params=pltpu.CompilerParams(vmem_limit_bytes=48 << 20),
        name="stack",
    )(me, bi, bj, bf, weights)


def whiten(records, usable):
    rows = records.shape[0]
    samples = records.reshape(rows, L).T
    even, odd = spectrum_tables()
    tables = (jnp.asarray(even), jnp.asarray(odd), jnp.asarray(window_ones()))
    vmem = pl.BlockSpec(memory_space=pltpu.VMEM)
    hbm = pl.BlockSpec(memory_space=pltpu.HBM)
    return pl.pallas_call(
        whiten_kernel,
        out_shape=(
            jax.ShapeDtypeStruct((CHUNKS, rows, 2 * CHUNK), jnp.bfloat16),
            jax.ShapeDtypeStruct((16, rows), jnp.bfloat16),
        ),
        in_specs=[vmem, vmem, hbm, hbm, hbm],
        out_specs=(vmem, vmem),
        scratch_shapes=[pltpu.VMEM(t.shape, t.dtype) for t in tables]
        + [pltpu.SemaphoreType.DMA((3,))],
        compiler_params=pltpu.CompilerParams(vmem_limit_bytes=63 << 20),
        name="whiten",
    )(samples, usable.reshape(1, rows), *tables)


def solution(mesh):
    pairs, hours = mesh.shape["pairs"], mesh.shape["hours"]
    width = 1 << ((pairs.bit_length() - 1) // 2)

    def body(records, usable, pair_blocks):
        whitened, marks = whiten(records, usable)
        asks = jnp.broadcast_to(
            pair_blocks.reshape(2, 1, 1).astype(jnp.float32), (2, 8, 128)
        )
        bj, bi, bf = exchange(pair_blocks, asks, whitened, marks, pairs, width, hours)
        me = lax.axis_index("hours").astype(jnp.int32).reshape(1)
        return stack(me, bi, bj, bf, jnp.asarray(lag_weights()))

    return jax.shard_map(
        body,
        mesh=mesh,
        in_specs=(P("pairs", "hours", None), P("pairs", "hours"), P("pairs", None)),
        out_specs=P("pairs", "hours", None, None),
        check_vma=False,
    )
```

```python
import functools
import math

import jax
import jax.numpy as jnp
import numpy as np
from jax import lax
from jax.experimental import pallas as pl
from jax.experimental.pallas import tpu as pltpu
from jax.sharding import PartitionSpec as P

L = 3600
F = 512
W = 32
F0 = 64
LAGS = 256
EXTENT = F + 2 * W
HALF = L // 2
HE = EXTENT // 2
HF = F // 2
CORES = 2
MESH = pl.DeviceIdType.MESH


def cos_sin(phases, length, scale):
    angles = np.float32(2.0 * math.pi / length) * (phases % length).astype(np.float32)
    wide = angles.astype(np.float64)
    scale = np.float32(scale)
    return np.cos(wide).astype(np.float32) * scale, -np.sin(wide).astype(np.float32) * scale


CHUNK = 256
CHUNKS = F // CHUNK


def spectrum_tables():
    bins = F0 - W + np.arange(EXTENT)
    c, q = cos_sin(bins[:, None] * np.arange(HALF)[None, :], L, 1.0 / math.sqrt(L))
    even = np.concatenate([c[0::2], q[0::2]], axis=0)
    odd = np.concatenate([c[1::2], q[1::2]], axis=0)
    return even.astype(jnp.bfloat16), odd.astype(jnp.bfloat16)


def window_ones():
    source = np.concatenate([np.arange(0, EXTENT, 2), np.arange(1, EXTENT, 2)])
    target = np.concatenate([np.arange(0, F, 2), np.arange(1, F, 2)])
    gap = source[None, :] - target[:, None]
    return ((gap >= 0) & (gap <= 2 * W)).astype(np.float32).astype(jnp.bfloat16)


def lag_weights():
    order = np.concatenate([np.arange(0, F, 2), np.arange(1, F, 2)])
    shifts = np.arange(LAGS) - LAGS // 2
    c, s = cos_sin((F0 + order)[:, None] * shifts[None, :], L, 1.0 / math.sqrt(F))
    pieces = []
    for k in range(0, F, CHUNK):
        pieces += [c[k : k + CHUNK], s[k : k + CHUNK]]
    return np.concatenate(pieces, axis=0).astype(jnp.bfloat16)


def split_hi_lo(value):
    high = value.astype(jnp.bfloat16)
    low = (value - high.astype(jnp.float32)).astype(jnp.bfloat16)
    return jnp.concatenate([high, low], axis=1)


def whiten_kernel(
    x_ref, use_ref, even_hbm, odd_hbm, ones_hbm, out_ref, even, odd, ones, sem
):
    stations = x_ref.shape[1]
    loads = [
        pltpu.make_async_copy(src, dst, sem.at[k])
        for k, (src, dst) in enumerate(((even_hbm, even), (odd_hbm, odd), (ones_hbm, ones)))
    ]
    for load in loads:
        load.start()
    flags = use_ref[...].astype(jnp.float32)
    early = x_ref[:HALF].astype(jnp.float32)
    late = x_ref[HALF:].astype(jnp.float32)

    def transform(load, table, signal):
        signal = split_hi_lo(signal)
        load.wait()
        both = jnp.dot(table[...], signal, preferred_element_type=jnp.float32)
        both = both[:, :stations] + both[:, stations:]
        return both[:HE], both[HE:]

    re_even, im_even = transform(loads[0], even, early + late)
    re_odd, im_odd = transform(loads[1], odd, early - late)
    power = jnp.concatenate(
        [re_even * re_even + im_even * im_even, re_odd * re_odd + im_odd * im_odd], axis=0
    )
    loads[2].wait()
    total = jnp.dot(ones[...], split_hi_lo(power), preferred_element_type=jnp.float32)
    smooth = (total[:, :stations] + total[:, stations:]) * jnp.float32(1.0 / (2 * W + 1))
    weight = flags / jnp.sqrt(smooth + 1e-05)
    w2 = W // 2
    for k in range(CHUNKS):
        at = k * CHUNK
        real, imag = (re_even, im_even) if at < HF else (re_odd, im_odd)
        inner = w2 + at % HF
        scale = weight[at : at + CHUNK]
        out_ref[k, :, :CHUNK] = (real[inner : inner + CHUNK] * scale).T.astype(jnp.bfloat16)
        out_ref[k, :, CHUNK:] = (imag[inner : inner + CHUNK] * scale).T.astype(jnp.bfloat16)


UNIT = 16
LAG = 1.6


def exchange_kernel(pairs, width, hours, pair_ref, use_ref, w_ref, bj, bi, ff, *scratch):
    rows = w_ref.shape[1]
    depth = pairs // width
    groups = hours // CORES
    part = rows // width
    peer_rows = rows // hours
    pieces = part // UNIT
    subs = peer_rows // UNIT
    units = CHUNKS * pieces
    base = depth * width
    pools, sels, picks = scratch[:units], scratch[units : 2 * units], scratch[2 * units : 3 * units]
    (
        asks, far, keep_sem, stay_sem, ask_send, ask_recv, far_send, far_recv,
        fh_send, fh_recv, fx_send, fx_recv, fz_send, fz_recv, f_local,
        cross_send, cross_recv, z_send, z_recv, sel_send, sel_recv, pick_send, pick_recv,
        i_send, i_recv, i_local, j_send, j_recv, relay_send,
    ) = scratch[3 * units :]
    p = lax.axis_index("pairs")
    me = lax.axis_index("hours")
    z, x = p // width, p % width
    y, core = me // CORES, me % CORES
    partner = y * CORES + (1 - core)
    middle = jnp.logical_and(z > 0, z < depth - 1)

    def beside(k):
        return (x + k + width) % width

    def span(u, at):
        c, q = u // pieces, u % pieces
        return c, pl.ds(pl.multiple_of(at * part + q * UNIT, UNIT), UNIT)

    barrier = pltpu.get_barrier_semaphore()
    for k in range(width):
        for h in range(hours):
            if k == 0 and h == 0:
                continue
            pl.semaphore_signal(
                barrier, inc=1,
                device_id={"pairs": z * width + beside(k), "hours": (me + h) % hours},
                device_id_type=MESH,
            )
    for k in range(1, depth):
        pl.semaphore_signal(
            barrier, inc=1, device_id={"pairs": ((z + k) % depth) * width + x},
            device_id_type=MESH,
        )
    pl.semaphore_wait(barrier, width * hours - 1 + depth - 1)

    pending = []

    def send(src, dst, send_sem, recv_sem, device_id, cond=None):
        def make():
            return pltpu.make_async_remote_copy(
                src_ref=src, dst_ref=dst, send_sem=send_sem, recv_sem=recv_sem,
                device_id=device_id, device_id_type=MESH,
            )

        if cond is None:
            make().start()
        else:
            @pl.when(cond)
            def _():
                make().start()
        pending.append((cond, make))

    def got(ref, sem):
        pltpu.make_async_remote_copy(
            src_ref=ref, dst_ref=ref, send_sem=sem, recv_sem=sem,
            device_id={"hours": me}, device_id_type=MESH,
        ).wait_recv()

    def stay(src, dst, sem):
        copy = pltpu.make_async_copy(src, dst, sem)
        copy.start()
        return copy

    for s in range(2):
        asks[x, 0, s] = pair_ref[0, s]
    for k in range(1, width):
        send(
            pair_ref, asks.at[x], ask_send.at[k], ask_recv.at[x],
            {"pairs": z * width + beside(k)},
        )
    own_flags = stay(use_ref, ff.at[p, me], f_local)
    for h in range(1, hours):
        send(
            use_ref, ff.at[p, me], fh_send.at[h], fh_recv.at[me], {"hours": (me + h) % hours}
        )
    keep = []
    for u in range(units):
        for k in range(1, width):
            send(
                w_ref.at[span(u, beside(k))], pools[u].at[p], cross_send.at[k, u],
                cross_recv.at[k, u], {"pairs": z * width + beside(k)},
            )
        keep.append(stay(w_ref.at[span(u, x)], pools[u].at[p], keep_sem.at[u]))

    def row_of(u, r):
        return pools[u].at[pl.ds(r * width, width)]

    def carry(u, r, way, cond):
        send(
            row_of(u, r), row_of(u, r), z_send.at[way, r, u], z_recv.at[r, u],
            {"pairs": p + (width if way == 0 else -width)}, cond,
        )

    def learn(_):
        for k in range(1, width):
            got(asks.at[beside(k)], ask_recv.at[beside(k)])
        send(asks, far.at[1], far_send.at[0], far_recv.at[1], {"pairs": p + width}, z == 0)
        send(asks, far.at[0], far_send.at[1], far_recv.at[0], {"pairs": p - width}, z == depth - 1)

    def flags_row(_):
        own_flags.wait()
        for h in range(1, hours):
            peer = (me + h) % hours
            got(ff.at[p, peer], fh_recv.at[peer])
        for k in range(1, width):
            send(
                ff.at[p], ff.at[p], fx_send.at[k], fx_recv.at[x],
                {"pairs": z * width + beside(k)},
            )

    def flags_column(_):
        for k in range(1, width):
            got(ff.at[z * width + beside(k)], fx_recv.at[beside(k)])
        mine = ff.at[pl.ds(z * width, width)]
        for k in range(1, depth):
            send(
                mine, mine, fz_send.at[k], fz_recv.at[z],
                {"pairs": ((z + k) % depth) * width + x},
            )

    def know(_):
        for way, at in ((0, depth - 2), (1, 1)):
            @pl.when(z == at)
            def _(way=way):
                got(far.at[way], far_recv.at[way])

    def own_row(u):
        keep[u].wait()
        for k in range(1, width):
            got(pools[u].at[z * width + beside(-k)], cross_recv.at[k, u])
        carry(u, z, 0, z < depth - 2)
        carry(u, z, 1, z > 1)

    def near_row(d, u):
        for way, r, here, on in (
            (0, z - d, jnp.logical_and(z - d >= 0, z < depth - 1), z < depth - 2),
            (1, z + d, jnp.logical_and(z + d < depth, z > 0), z > 1),
        ):
            @pl.when(here)
            def _(r=r):
                got(row_of(u, r), z_recv.at[r, u])
            carry(u, r, way, jnp.logical_and(here, on))
        if d == depth - 2:
            for way, at in ((0, depth - 2), (1, 1)):
                @pl.when(z == at)
                def _(way=way):
                    for x2 in range(width):
                        for s in range(2):
                            sels[u][way, 2 * x2 + s] = pools[u][far[way, x2, 0, s]]
                send(
                    sels[u].at[way], pools[u].at[pl.ds(base, 2 * width)], sel_send.at[way, u],
                    sel_recv.at[u], {"pairs": p + (width if way == 0 else -width)}, z == at,
                )

    def pick(u):
        @pl.when(jnp.logical_not(middle))
        def _():
            got(pools[u].at[pl.ds(base, 2 * width)], sel_recv.at[u])
        c, mine = span(u, x)
        q = u % pieces
        for k in range(width):
            x2 = beside(-k)
            for s in range(2):
                b = asks[x2, 0, s]
                away = jnp.logical_and(jnp.logical_not(middle), lax.div(b, width) != z)
                picks[u][k, s] = pools[u][jnp.where(away, base + 2 * x2 + s, b)]
        for k in range(1, width):
            send(
                picks[u].at[k, 1], bj.at[me, c, mine], pick_send.at[k, u], pick_recv.at[k, u],
                {"pairs": z * width + beside(-k)},
            )
        share(u, 0, picks[u].at[0, 1])
        peer = x * (part // peer_rows) + q * UNIT // peer_rows
        sub = (q * UNIT % peer_rows) // UNIT
        land = bi.at[me, c, pl.ds(sub * UNIT, UNIT)]
        for k in range(width):
            send(
                picks[u].at[k, 0], land, i_send.at[k, u], i_recv.at[me, c, sub],
                {"pairs": z * width + beside(-k), "hours": peer}, None if k else me != peer,
            )

        @pl.when(me == peer)
        def _():
            stay(picks[u].at[0, 0], land, i_local.at[c, sub])
        stays.append(stay(picks[u].at[0, 1], bj.at[me, c, mine], stay_sem.at[u]))

    stays = []

    def share(u, k, src):
        c, at = span(u, beside(k))
        for g in range(1, groups):
            send(
                src, bj.at[me, c, at], j_send.at[g, k, u], j_recv.at[me, k, u],
                {"hours": ((y + g) % groups) * CORES + core},
            )
        send(src, bj.at[me, c, at], j_send.at[0, k, u], j_recv.at[me, k, u], {"hours": partner})

    def share_row(u):
        for k in range(1, width):
            c, at = span(u, beside(k))
            got(bj.at[me, c, at], pick_recv.at[k, u])
            share(u, k, bj.at[me, c, at])

    def relay(u):
        for k in range(width):
            c, at = span(u, beside(k))
            for g in range(1, groups):
                peer = ((y + g) % groups) * CORES + core
                piece = bj.at[peer, c, at]
                got(piece, j_recv.at[peer, k, u])
                send(
                    piece, piece, relay_send.at[g, k, u], j_recv.at[peer, k, u],
                    {"hours": partner},
                )

    steps = [(0.0, learn, 0), (LAG + 0.1, flags_row, 0), (2 * LAG + 0.1, flags_column, 0)]
    steps.append((2 * LAG + 0.2, know, 0))
    stages = [own_row]
    stages += [functools.partial(near_row, d) for d in range(1, depth - 1)]
    stages += [pick, share_row, relay]
    for n, stage in enumerate(stages):
        for u in range(units):
            steps.append(((n + 1) * LAG + u, stage, u))
    for _, stage, u in sorted(steps, key=lambda step: step[0]):
        stage(u)

    for u in range(units):
        for k in range(width):
            c, at = span(u, beside(k))
            for g in range(groups):
                peer = ((y + g) % groups) * CORES + (1 - core)
                got(bj.at[peer, c, at], j_recv.at[peer, k, u])
    near = x == me // (part // peer_rows)
    for h in range(hours):
        hour = (me + h) % hours
        for c in range(CHUNKS):
            for sub in range(subs):
                land = bi.at[hour, c, pl.ds(sub * UNIT, UNIT)]
                if h:
                    got(land, i_recv.at[hour, c, sub])
                    continue

                @pl.when(jnp.logical_not(near))
                def _(land=land, c=c, sub=sub):
                    got(land, i_recv.at[me, c, sub])

                @pl.when(near)
                def _(land=land, c=c, sub=sub):
                    pltpu.make_async_copy(land, land, i_local.at[c, sub]).wait()
    for k in range(1, depth):
        r = (z + k) % depth
        got(ff.at[pl.ds(r * width, width)], fz_recv.at[r])
    for copy in stays:
        copy.wait()
    for cond, make in pending:
        if cond is None:
            make().wait_send()
        else:
            @pl.when(cond)
            def _(make=make):
                make().wait_send()


def exchange(pair_blocks, flags, whitened, pairs, width, hours):
    rows, cols = whitened.shape[1:]
    part = rows // hours
    units = CHUNKS * (rows // width // UNIT)
    any_space = pl.BlockSpec(memory_space=pl.ANY)
    smem = pl.BlockSpec(memory_space=pltpu.SMEM)
    dma = pltpu.SemaphoreType.DMA
    groups = hours // CORES
    depth = pairs // width
    bf16 = jnp.bfloat16
    return pl.pallas_call(
        functools.partial(exchange_kernel, pairs, width, hours),
        out_shape=(
            jax.ShapeDtypeStruct((hours, CHUNKS, rows, cols), bf16),
            jax.ShapeDtypeStruct((hours, CHUNKS, part, cols), bf16),
            jax.ShapeDtypeStruct((pairs, hours) + flags.shape, flags.dtype),
        ),
        in_specs=[smem, any_space, any_space],
        out_specs=(any_space, any_space, any_space),
        scratch_shapes=[pltpu.VMEM((depth * width + 2 * width, UNIT, cols), bf16)] * units
        + [pltpu.VMEM((2, 2 * width, UNIT, cols), bf16)] * units
        + [pltpu.VMEM((width, 2, UNIT, cols), bf16)] * units
        + [
            pltpu.SMEM((width, 1, 2), jnp.int32),
            pltpu.SMEM((2, width, 1, 2), jnp.int32),
            dma((units,)),
            dma((units,)),
            dma((width,)),
            dma((width,)),
            dma((2,)),
            dma((2,)),
            dma((hours,)),
            dma((hours,)),
            dma((width,)),
            dma((width,)),
            dma((depth,)),
            dma((depth,)),
            dma(()),
            dma((width, units)),
            dma((width, units)),
            dma((2, depth, units)),
            dma((depth, units)),
            dma((2, units)),
            dma((units,)),
            dma((width, units)),
            dma((width, units)),
            dma((width, units)),
            dma((hours, CHUNKS, part // UNIT)),
            dma((CHUNKS, part // UNIT)),
            dma((groups, width, units)),
            dma((hours, width, units)),
            dma((groups, width, units)),
        ],
        compiler_params=pltpu.CompilerParams(
            collective_id=0, has_side_effects=True, vmem_limit_bytes=32 << 20
        ),
        name="exchange",
    )(pair_blocks, flags, whitened)


GROUP = 8
SUB = 2
BLOCK = 8


def stack_kernel(
    hours, me_ref, pair_ref, bi_ref, bj_ref, ff_ref, g_ref, out_ref, af, heads, recip, *cross
):
    step = pl.program_id(0)
    rows = bj_ref.shape[2]
    first_rows = bi_ref.shape[2]
    f32 = jnp.float32

    @pl.when(step == 0)
    def _():
        af[...] = bi_ref[...].astype(f32)
        first = ff_ref[pair_ref[0, 0], :, 0, :].astype(f32)
        second = ff_ref[pair_ref[0, 1], :, 0, :].astype(f32)
        counts = lax.dot_general(
            second, first, (((0,), (0,)), ((), ())), preferred_element_type=f32
        )
        recip[...] = 1.0 / jnp.maximum(counts, 1.0)

    offset = me_ref[0] * first_rows + step * GROUP
    scale = pltpu.roll(recip[...], (rows - offset) % rows, 1)
    at_rows = pl.ds(pl.multiple_of(step * GROUP, GROUP), GROUP)
    for h in range(hours):
        for c in range(CHUNKS):
            ar = af[h, c, at_rows, :CHUNK]
            ai = af[h, c, at_rows, CHUNK:]
            for k, value in enumerate((ar, ai)):
                for a in range(GROUP):
                    heads[a, c, h, k] = jnp.broadcast_to(
                        value[a : a + 1], (BLOCK, CHUNK)
                    ).astype(jnp.bfloat16)

    for sub in range(GROUP // SUB):
        buf = cross[sub]
        for c in range(CHUNKS):
            lo = 2 * CHUNK * c
            hi = lo + CHUNK
            for r in range(0, rows, BLOCK):
                tails = []
                for h in range(hours):
                    tails.append(
                        (
                            bj_ref[h, c, r : r + BLOCK, :CHUNK],
                            bj_ref[h, c, r : r + BLOCK, CHUNK:],
                        )
                    )
                for a in range(SUB):
                    real = imag = None
                    for h in range(hours):
                        ar, ai = heads[sub * SUB + a, c, h, 0], heads[sub * SUB + a, c, h, 1]
                        br, bm = tails[h]
                        re = ar * br + ai * bm
                        im = ai * br - ar * bm
                        real = re if real is None else real + re
                        imag = im if imag is None else imag + im
                    at = a * rows + r
                    buf[at : at + BLOCK, lo:hi] = real
                    buf[at : at + BLOCK, hi : hi + CHUNK] = imag
        lagged = jnp.dot(buf[...], g_ref[...], preferred_element_type=f32)
        for a in range(SUB):
            k = sub * SUB + a
            out_ref[0, k] = lagged[a * rows : (a + 1) * rows] * scale[:, k : k + 1]


def stack(me, pair_blocks, bi, bj, ff, weights):
    hours, _, first_rows, cols = bi.shape
    rows = bj.shape[2]
    full = lambda a: pl.BlockSpec(a.shape, lambda i, *_: (0,) * a.ndim, pipeline_mode=pl.Buffered(1))
    return pl.pallas_call(
        functools.partial(stack_kernel, hours),
        grid_spec=pltpu.PrefetchScalarGridSpec(
            num_scalar_prefetch=2,
            grid=(first_rows // GROUP,),
            in_specs=[full(bi), full(bj), full(ff), full(weights)],
            out_specs=pl.BlockSpec((1, GROUP, rows, LAGS), lambda i, *_: (0, i, 0, 0)),
            scratch_shapes=[
                pltpu.VMEM((hours, CHUNKS, first_rows, cols), jnp.float32),
                pltpu.VMEM((GROUP, CHUNKS, hours, 2, BLOCK, CHUNK), jnp.bfloat16),
                pltpu.VMEM((rows, rows), jnp.float32),
            ]
            + [pltpu.VMEM((SUB * rows, 2 * F), jnp.bfloat16)] * (GROUP // SUB),
        ),
        out_shape=jax.ShapeDtypeStruct((1, first_rows, rows, LAGS), jnp.float32),
        compiler_params=pltpu.CompilerParams(vmem_limit_bytes=48 << 20),
        name="stack",
    )(me, pair_blocks, bi, bj, ff, weights)


def whiten(records, usable):
    rows = records.shape[0]
    samples = records.reshape(rows, L).T
    even, odd = spectrum_tables()
    tables = (jnp.asarray(even), jnp.asarray(odd), jnp.asarray(window_ones()))
    vmem = pl.BlockSpec(memory_space=pltpu.VMEM)
    hbm = pl.BlockSpec(memory_space=pltpu.HBM)
    return pl.pallas_call(
        whiten_kernel,
        out_shape=jax.ShapeDtypeStruct((CHUNKS, rows, 2 * CHUNK), jnp.bfloat16),
        in_specs=[vmem, vmem, hbm, hbm, hbm],
        out_specs=vmem,
        scratch_shapes=[pltpu.VMEM(t.shape, t.dtype) for t in tables]
        + [pltpu.SemaphoreType.DMA((3,))],
        compiler_params=pltpu.CompilerParams(vmem_limit_bytes=63 << 20),
        name="whiten",
    )(samples, usable.reshape(1, rows), *tables)


def solution(mesh):
    pairs, hours = mesh.shape["pairs"], mesh.shape["hours"]
    width = 1 << ((pairs.bit_length() - 1) // 2)

    def body(records, usable, pair_blocks):
        whitened = whiten(records, usable)
        flags = usable.reshape(1, usable.shape[0])
        bj, bi, ff = exchange(pair_blocks, flags, whitened, pairs, width, hours)
        me = lax.axis_index("hours").astype(jnp.int32).reshape(1)
        return stack(me, pair_blocks, bi, bj, ff, jnp.asarray(lag_weights()))

    return jax.shard_map(
        body,
        mesh=mesh,
        in_specs=(P("pairs", "hours", None), P("pairs", "hours"), P("pairs", None)),
        out_specs=P("pairs", "hours", None, None),
        check_vma=False,
    )
```

```python
import functools
import math

import jax
import jax.numpy as jnp
import numpy as np
from jax import lax
from jax.experimental import pallas as pl
from jax.experimental.pallas import tpu as pltpu
from jax.sharding import PartitionSpec as P

L = 3600
F = 512
W = 32
F0 = 64
LAGS = 256
EXTENT = F + 2 * W
HALF = L // 2
HE = EXTENT // 2
HF = F // 2
CORES = 2
MESH = pl.DeviceIdType.MESH


def cos_sin(phases, length, scale):
    angles = np.float32(2.0 * math.pi / length) * (phases % length).astype(np.float32)
    wide = angles.astype(np.float64)
    scale = np.float32(scale)
    return np.cos(wide).astype(np.float32) * scale, -np.sin(wide).astype(np.float32) * scale


CHUNK = 256
CHUNKS = F // CHUNK


def spectrum_tables():
    bins = F0 - W + np.arange(EXTENT)
    c, q = cos_sin(bins[:, None] * np.arange(HALF)[None, :], L, 1.0 / math.sqrt(L))
    even = np.concatenate([c[0::2], q[0::2]], axis=0)
    odd = np.concatenate([c[1::2], q[1::2]], axis=0)
    return even.astype(jnp.bfloat16), odd.astype(jnp.bfloat16)


def window_ones():
    source = np.concatenate([np.arange(0, EXTENT, 2), np.arange(1, EXTENT, 2)])
    target = np.concatenate([np.arange(0, F, 2), np.arange(1, F, 2)])
    gap = source[None, :] - target[:, None]
    return ((gap >= 0) & (gap <= 2 * W)).astype(np.float32).astype(jnp.bfloat16)


def lag_weights():
    order = np.concatenate([np.arange(0, F, 2), np.arange(1, F, 2)])
    shifts = np.arange(LAGS) - LAGS // 2
    c, s = cos_sin((F0 + order)[:, None] * shifts[None, :], L, 1.0 / math.sqrt(F))
    pieces = []
    for k in range(0, F, CHUNK):
        pieces += [c[k : k + CHUNK], s[k : k + CHUNK]]
    return np.concatenate(pieces, axis=0).astype(jnp.bfloat16)


def split_hi_lo(value):
    high = value.astype(jnp.bfloat16)
    low = (value - high.astype(jnp.float32)).astype(jnp.bfloat16)
    return jnp.concatenate([high, low], axis=1)


def whiten(x_ref, use_ref, even, odd, ones, w_ref, loads):
    stations = x_ref.shape[1]
    loads[4].wait()
    flags = use_ref[...].astype(jnp.float32)
    loads[0].wait()
    early = x_ref[:HALF].astype(jnp.float32)
    late = x_ref[HALF:].astype(jnp.float32)

    def transform(load, table, signal):
        signal = split_hi_lo(signal)
        load.wait()
        both = jnp.dot(table[...], signal, preferred_element_type=jnp.float32)
        both = both[:, :stations] + both[:, stations:]
        return both[:HE], both[HE:]

    re_even, im_even = transform(loads[1], even, early + late)
    re_odd, im_odd = transform(loads[2], odd, early - late)
    power = jnp.concatenate(
        [re_even * re_even + im_even * im_even, re_odd * re_odd + im_odd * im_odd], axis=0
    )
    loads[3].wait()
    total = jnp.dot(ones[...], split_hi_lo(power), preferred_element_type=jnp.float32)
    smooth = (total[:, :stations] + total[:, stations:]) * jnp.float32(1.0 / (2 * W + 1))
    weight = flags / jnp.sqrt(smooth + 1e-05)
    w2 = W // 2
    for k in range(CHUNKS):
        at = k * CHUNK
        real, imag = (re_even, im_even) if at < HF else (re_odd, im_odd)
        inner = w2 + at % HF
        scale = weight[at : at + CHUNK]
        w_ref[k, :, :CHUNK] = (real[inner : inner + CHUNK] * scale).T.astype(jnp.bfloat16)
        w_ref[k, :, CHUNK:] = (imag[inner : inner + CHUNK] * scale).T.astype(jnp.bfloat16)


UNIT = 16
LAG = 3.2


def exchange_kernel(
    pairs, width, hours, pair_ref, use_hbm, x_hbm, even_hbm, odd_hbm, ones_hbm, bj, bi, ff,
    use_ref, x_ref, even, odd, ones, load_sem, w_ref, *scratch
):
    loads = [
        pltpu.make_async_copy(src, dst, load_sem.at[k])
        for k, (src, dst) in enumerate(
            (
                (x_hbm, x_ref), (even_hbm, even), (odd_hbm, odd), (ones_hbm, ones),
                (use_hbm, use_ref),
            )
        )
    ]
    for load in loads:
        load.start()
    rows = w_ref.shape[1]
    depth = pairs // width
    groups = hours // CORES
    part = rows // width
    peer_rows = rows // hours
    pieces = part // UNIT
    subs = peer_rows // UNIT
    units = CHUNKS * pieces
    base = depth * width
    pools, sels, picks = scratch[:units], scratch[units : 2 * units], scratch[2 * units : 3 * units]
    (
        asks, far, keep_sem, stay_sem, ask_send, ask_recv, far_send, far_recv,
        fh_send, fh_recv, fx_send, fx_recv, fz_send, fz_recv, f_local,
        cross_send, cross_recv, z_send, z_recv, sel_send, sel_recv, pick_send, pick_recv,
        i_send, i_recv, i_local, j_send, j_recv, relay_send,
    ) = scratch[3 * units :]
    p = lax.axis_index("pairs")
    me = lax.axis_index("hours")
    z, x = p // width, p % width
    y, core = me // CORES, me % CORES
    partner = y * CORES + (1 - core)
    middle = jnp.logical_and(z > 0, z < depth - 1)

    def beside(k):
        return (x + k + width) % width

    def span(u, at):
        c, q = u // pieces, u % pieces
        return c, pl.ds(pl.multiple_of(at * part + q * UNIT, UNIT), UNIT)

    barrier = pltpu.get_barrier_semaphore()
    for k in range(width):
        for h in range(hours):
            if k == 0 and h == 0:
                continue
            pl.semaphore_signal(
                barrier, inc=1,
                device_id={"pairs": z * width + beside(k), "hours": (me + h) % hours},
                device_id_type=MESH,
            )
    for k in range(1, depth):
        pl.semaphore_signal(
            barrier, inc=1, device_id={"pairs": ((z + k) % depth) * width + x},
            device_id_type=MESH,
        )
    whiten(x_ref, use_ref, even, odd, ones, w_ref, loads)
    pl.semaphore_wait(barrier, width * hours - 1 + depth - 1)

    pending = []

    def send(src, dst, send_sem, recv_sem, device_id, cond=None):
        def make():
            return pltpu.make_async_remote_copy(
                src_ref=src, dst_ref=dst, send_sem=send_sem, recv_sem=recv_sem,
                device_id=device_id, device_id_type=MESH,
            )

        if cond is None:
            make().start()
        else:
            @pl.when(cond)
            def _():
                make().start()
        pending.append((cond, make))

    def got(ref, sem):
        pltpu.make_async_remote_copy(
            src_ref=ref, dst_ref=ref, send_sem=sem, recv_sem=sem,
            device_id={"hours": me}, device_id_type=MESH,
        ).wait_recv()

    def stay(src, dst, sem):
        copy = pltpu.make_async_copy(src, dst, sem)
        copy.start()
        return copy

    for s in range(2):
        asks[x, 0, s] = pair_ref[0, s]
    for k in range(1, width):
        send(
            pair_ref, asks.at[x], ask_send.at[k], ask_recv.at[x],
            {"pairs": z * width + beside(k)},
        )
    own_flags = stay(use_ref, ff.at[p, me], f_local)
    for h in range(1, hours):
        send(
            use_ref, ff.at[p, me], fh_send.at[h], fh_recv.at[me], {"hours": (me + h) % hours}
        )
    keep = []
    for u in range(units):
        for k in range(1, width):
            send(
                w_ref.at[span(u, beside(k))], pools[u].at[p], cross_send.at[k, u],
                cross_recv.at[k, u], {"pairs": z * width + beside(k)},
            )
        keep.append(stay(w_ref.at[span(u, x)], pools[u].at[p], keep_sem.at[u]))

    def row_of(u, r):
        return pools[u].at[pl.ds(r * width, width)]

    def carry(u, r, way, cond):
        send(
            row_of(u, r), row_of(u, r), z_send.at[way, r, u], z_recv.at[r, u],
            {"pairs": p + (width if way == 0 else -width)}, cond,
        )

    def learn(_):
        for k in range(1, width):
            got(asks.at[beside(k)], ask_recv.at[beside(k)])
        send(asks, far.at[1], far_send.at[0], far_recv.at[1], {"pairs": p + width}, z == 0)
        send(asks, far.at[0], far_send.at[1], far_recv.at[0], {"pairs": p - width}, z == depth - 1)

    def flags_row(_):
        own_flags.wait()
        for h in range(1, hours):
            peer = (me + h) % hours
            got(ff.at[p, peer], fh_recv.at[peer])
        for k in range(1, width):
            send(
                ff.at[p], ff.at[p], fx_send.at[k], fx_recv.at[x],
                {"pairs": z * width + beside(k)},
            )

    def flags_column(_):
        for k in range(1, width):
            got(ff.at[z * width + beside(k)], fx_recv.at[beside(k)])
        mine = ff.at[pl.ds(z * width, width)]
        for k in range(1, depth):
            send(
                mine, mine, fz_send.at[k], fz_recv.at[z],
                {"pairs": ((z + k) % depth) * width + x},
            )

    def know(_):
        for way, at in ((0, depth - 2), (1, 1)):
            @pl.when(z == at)
            def _(way=way):
                got(far.at[way], far_recv.at[way])

    def own_row(u):
        keep[u].wait()
        for k in range(1, width):
            got(pools[u].at[z * width + beside(-k)], cross_recv.at[k, u])
        carry(u, z, 0, z < depth - 2)
        carry(u, z, 1, z > 1)

    def near_row(d, u):
        for way, r, here, on in (
            (0, z - d, jnp.logical_and(z - d >= 0, z < depth - 1), z < depth - 2),
            (1, z + d, jnp.logical_and(z + d < depth, z > 0), z > 1),
        ):
            @pl.when(here)
            def _(r=r):
                got(row_of(u, r), z_recv.at[r, u])
            carry(u, r, way, jnp.logical_and(here, on))
        if d == depth - 2:
            for way, at in ((0, depth - 2), (1, 1)):
                @pl.when(z == at)
                def _(way=way):
                    for x2 in range(width):
                        for s in range(2):
                            sels[u][way, 2 * x2 + s] = pools[u][far[way, x2, 0, s]]
                send(
                    sels[u].at[way], pools[u].at[pl.ds(base, 2 * width)], sel_send.at[way, u],
                    sel_recv.at[u], {"pairs": p + (width if way == 0 else -width)}, z == at,
                )

    def pick(u):
        @pl.when(jnp.logical_not(middle))
        def _():
            got(pools[u].at[pl.ds(base, 2 * width)], sel_recv.at[u])
        c, mine = span(u, x)
        q = u % pieces
        for k in range(width):
            x2 = beside(-k)
            for s in range(2):
                b = asks[x2, 0, s]
                away = jnp.logical_and(jnp.logical_not(middle), lax.div(b, width) != z)
                picks[u][k, s] = pools[u][jnp.where(away, base + 2 * x2 + s, b)]
        for k in range(1, width):
            send(
                picks[u].at[k, 1], bj.at[me, c, mine], pick_send.at[k, u], pick_recv.at[k, u],
                {"pairs": z * width + beside(-k)},
            )
        share(u, 0, picks[u].at[0, 1])
        peer = x * (part // peer_rows) + q * UNIT // peer_rows
        sub = (q * UNIT % peer_rows) // UNIT
        land = bi.at[me, c, pl.ds(sub * UNIT, UNIT)]
        for k in range(width):
            send(
                picks[u].at[k, 0], land, i_send.at[k, u], i_recv.at[me, c, sub],
                {"pairs": z * width + beside(-k), "hours": peer}, None if k else me != peer,
            )

        @pl.when(me == peer)
        def _():
            stay(picks[u].at[0, 0], land, i_local.at[c, sub])
        stays.append(stay(picks[u].at[0, 1], bj.at[me, c, mine], stay_sem.at[u]))

    stays = []

    def share(u, k, src):
        c, at = span(u, beside(k))
        for g in range(1, groups):
            send(
                src, bj.at[me, c, at], j_send.at[g, k, u], j_recv.at[me, k, u],
                {"hours": ((y + g) % groups) * CORES + core},
            )
        send(src, bj.at[me, c, at], j_send.at[0, k, u], j_recv.at[me, k, u], {"hours": partner})

    def share_row(u):
        for k in range(1, width):
            c, at = span(u, beside(k))
            got(bj.at[me, c, at], pick_recv.at[k, u])
            share(u, k, bj.at[me, c, at])

    def relay(u):
        for k in range(width):
            c, at = span(u, beside(k))
            for g in range(1, groups):
                peer = ((y + g) % groups) * CORES + core
                piece = bj.at[peer, c, at]
                got(piece, j_recv.at[peer, k, u])
                send(
                    piece, piece, relay_send.at[g, k, u], j_recv.at[peer, k, u],
                    {"hours": partner},
                )

    steps = [(0.0, learn, 0), (4.0 * LAG, flags_row, 0), (units + 3.0 * LAG, flags_column, 0)]
    steps.append((2 * LAG + 0.2, know, 0))
    stages = [own_row]
    stages += [functools.partial(near_row, d) for d in range(1, depth - 1)]
    stages += [pick, share_row, relay]
    for n, stage in enumerate(stages):
        for u in range(units):
            steps.append(((n + 1) * LAG + u, stage, u))
    for _, stage, u in sorted(steps, key=lambda step: step[0]):
        stage(u)

    for u in range(units):
        for k in range(width):
            c, at = span(u, beside(k))
            for g in range(groups):
                peer = ((y + g) % groups) * CORES + (1 - core)
                got(bj.at[peer, c, at], j_recv.at[peer, k, u])
    near = x == me // (part // peer_rows)
    for h in range(hours):
        hour = (me + h) % hours
        for c in range(CHUNKS):
            for sub in range(subs):
                land = bi.at[hour, c, pl.ds(sub * UNIT, UNIT)]
                if h:
                    got(land, i_recv.at[hour, c, sub])
                    continue

                @pl.when(jnp.logical_not(near))
                def _(land=land, c=c, sub=sub):
                    got(land, i_recv.at[me, c, sub])

                @pl.when(near)
                def _(land=land, c=c, sub=sub):
                    pltpu.make_async_copy(land, land, i_local.at[c, sub]).wait()
    for k in range(1, depth):
        r = (z + k) % depth
        got(ff.at[pl.ds(r * width, width)], fz_recv.at[r])
    for copy in stays:
        copy.wait()
    for cond, make in pending:
        if cond is None:
            make().wait_send()
        else:
            @pl.when(cond)
            def _(make=make):
                make().wait_send()


def exchange(pair_blocks, usable, records, pairs, width, hours):
    rows = records.shape[0]
    samples = records.reshape(rows, L).T
    flags = usable.reshape(1, rows)
    tables = tuple(jnp.asarray(t) for t in (*spectrum_tables(), window_ones()))
    cols = 2 * CHUNK
    part = rows // hours
    units = CHUNKS * (rows // width // UNIT)
    any_space = pl.BlockSpec(memory_space=pl.ANY)
    smem = pl.BlockSpec(memory_space=pltpu.SMEM)
    dma = pltpu.SemaphoreType.DMA
    groups = hours // CORES
    depth = pairs // width
    bf16 = jnp.bfloat16
    return pl.pallas_call(
        functools.partial(exchange_kernel, pairs, width, hours),
        out_shape=(
            jax.ShapeDtypeStruct((hours, CHUNKS, rows, cols), bf16),
            jax.ShapeDtypeStruct((hours, CHUNKS, part, cols), bf16),
            jax.ShapeDtypeStruct((pairs, hours) + flags.shape, flags.dtype),
        ),
        in_specs=[smem] + [pl.BlockSpec(memory_space=pltpu.HBM)] * 5,
        out_specs=(any_space, any_space, any_space),
        scratch_shapes=[pltpu.VMEM(t.shape, t.dtype) for t in (flags, samples, *tables)]
        + [dma((5,)), pltpu.VMEM((CHUNKS, rows, cols), bf16)]
        + [pltpu.VMEM((depth * width + 2 * width, UNIT, cols), bf16)] * units
        + [pltpu.VMEM((2, 2 * width, UNIT, cols), bf16)] * units
        + [pltpu.VMEM((width, 2, UNIT, cols), bf16)] * units
        + [
            pltpu.SMEM((width, 1, 2), jnp.int32),
            pltpu.SMEM((2, width, 1, 2), jnp.int32),
            dma((units,)),
            dma((units,)),
            dma((width,)),
            dma((width,)),
            dma((2,)),
            dma((2,)),
            dma((hours,)),
            dma((hours,)),
            dma((width,)),
            dma((width,)),
            dma((depth,)),
            dma((depth,)),
            dma(()),
            dma((width, units)),
            dma((width, units)),
            dma((2, depth, units)),
            dma((depth, units)),
            dma((2, units)),
            dma((units,)),
            dma((width, units)),
            dma((width, units)),
            dma((width, units)),
            dma((hours, CHUNKS, part // UNIT)),
            dma((CHUNKS, part // UNIT)),
            dma((groups, width, units)),
            dma((hours, width, units)),
            dma((groups, width, units)),
        ],
        compiler_params=pltpu.CompilerParams(
            collective_id=0, has_side_effects=True, vmem_limit_bytes=48 << 20
        ),
        name="exchange",
    )(
        pair_blocks,
        *(pltpu.with_memory_space_constraint(t, pltpu.HBM) for t in (flags, samples, *tables)),
    )


GROUP = 8
SUB = 2
BLOCK = 8


def stack_kernel(
    hours, me_ref, pair_ref, bi_ref, bj_ref, ff_ref, g_ref, out_ref, af, heads, recip, *cross
):
    step = pl.program_id(0)
    rows = bj_ref.shape[2]
    first_rows = bi_ref.shape[2]
    f32 = jnp.float32

    @pl.when(step == 0)
    def _():
        af[...] = bi_ref[...].astype(f32)
        first = ff_ref[pair_ref[0, 0], :, 0, :].astype(f32)
        second = ff_ref[pair_ref[0, 1], :, 0, :].astype(f32)
        counts = lax.dot_general(
            second, first, (((0,), (0,)), ((), ())), preferred_element_type=f32
        )
        recip[...] = 1.0 / jnp.maximum(counts, 1.0)

    offset = me_ref[0] * first_rows + step * GROUP
    scale = pltpu.roll(recip[...], (rows - offset) % rows, 1)
    at_rows = pl.ds(pl.multiple_of(step * GROUP, GROUP), GROUP)
    for h in range(hours):
        for c in range(CHUNKS):
            ar = af[h, c, at_rows, :CHUNK]
            ai = af[h, c, at_rows, CHUNK:]
            for k, value in enumerate((ar, ai)):
                for a in range(GROUP):
                    heads[a, c, h, k] = jnp.broadcast_to(
                        value[a : a + 1], (BLOCK, CHUNK)
                    ).astype(jnp.bfloat16)

    for sub in range(GROUP // SUB):
        buf = cross[sub]
        for c in range(CHUNKS):
            lo = 2 * CHUNK * c
            hi = lo + CHUNK
            for r in range(0, rows, BLOCK):
                tails = []
                for h in range(hours):
                    tails.append(
                        (
                            bj_ref[h, c, r : r + BLOCK, :CHUNK],
                            bj_ref[h, c, r : r + BLOCK, CHUNK:],
                        )
                    )
                for a in range(SUB):
                    real = imag = None
                    for h in range(hours):
                        ar, ai = heads[sub * SUB + a, c, h, 0], heads[sub * SUB + a, c, h, 1]
                        br, bm = tails[h]
                        re = ar * br + ai * bm
                        im = ai * br - ar * bm
                        real = re if real is None else real + re
                        imag = im if imag is None else imag + im
                    at = a * rows + r
                    buf[at : at + BLOCK, lo:hi] = real
                    buf[at : at + BLOCK, hi : hi + CHUNK] = imag
        lagged = jnp.dot(buf[...], g_ref[...], preferred_element_type=f32)
        for a in range(SUB):
            k = sub * SUB + a
            out_ref[0, k] = lagged[a * rows : (a + 1) * rows] * scale[:, k : k + 1]


def stack(me, pair_blocks, bi, bj, ff, weights):
    hours, _, first_rows, cols = bi.shape
    rows = bj.shape[2]
    full = lambda a: pl.BlockSpec(a.shape, lambda i, *_: (0,) * a.ndim, pipeline_mode=pl.Buffered(1))
    return pl.pallas_call(
        functools.partial(stack_kernel, hours),
        grid_spec=pltpu.PrefetchScalarGridSpec(
            num_scalar_prefetch=2,
            grid=(first_rows // GROUP,),
            in_specs=[full(bi), full(bj), full(ff), full(weights)],
            out_specs=pl.BlockSpec((1, GROUP, rows, LAGS), lambda i, *_: (0, i, 0, 0)),
            scratch_shapes=[
                pltpu.VMEM((hours, CHUNKS, first_rows, cols), jnp.float32),
                pltpu.VMEM((GROUP, CHUNKS, hours, 2, BLOCK, CHUNK), jnp.bfloat16),
                pltpu.VMEM((rows, rows), jnp.float32),
            ]
            + [pltpu.VMEM((SUB * rows, 2 * F), jnp.bfloat16)] * (GROUP // SUB),
        ),
        out_shape=jax.ShapeDtypeStruct((1, first_rows, rows, LAGS), jnp.float32),
        compiler_params=pltpu.CompilerParams(vmem_limit_bytes=48 << 20),
        name="stack",
    )(me, pair_blocks, bi, bj, ff, weights)


def solution(mesh):
    pairs, hours = mesh.shape["pairs"], mesh.shape["hours"]
    width = 1 << ((pairs.bit_length() - 1) // 2)

    def body(records, usable, pair_blocks):
        bj, bi, ff = exchange(pair_blocks, usable, records, pairs, width, hours)
        me = lax.axis_index("hours").astype(jnp.int32).reshape(1)
        return stack(me, pair_blocks, bi, bj, ff, jnp.asarray(lag_weights()))

    return jax.shard_map(
        body,
        mesh=mesh,
        in_specs=(P("pairs", "hours", None), P("pairs", "hours"), P("pairs", None)),
        out_specs=P("pairs", "hours", None, None),
        check_vma=False,
    )
```
